32 devices in a mesh: chan: 2 (over y), tile: 16 (over z, x, core).
Axes of the slice: x: 2, y: 2, z: 4, core: 2. Of those that a mesh axis runs over, the one named last changes fastest.
Arguments:
- sky_cube: float32 [256, 512, 1024], P('chan', 'tile'), may hold values from -8 to 8
- pixel_mask: int32 [512, 1024], P('tile'), may hold values 0 or 1
- radius: int32 [256], replicated, may hold values from 1 to 4, as said below
- chan_weight: float32 [256], replicated, may hold values from 0.5 to 2
- band: float32 [17, 256], replicated, may hold values from -0.15 to 0.15
- resample: float32 [256, 256], replicated, may hold values from -0.375 to 0.375
- slab_index: int32 [256], replicated, may hold values from 0 to 15, never falling along the last dimension, each value on 1 to 20 neighbouring positions
Outputs:
- slabs: float32 [320, 512, 1024], P('tile', None, 'chan')
The draws below stay inside these ranges and needn't reach their ends.
Inputs may be any that keep to these rules, and one draw needn't show every extreme that they name: Every channel's radius is 1 to 4; some channel has 4. `slab_index`: never falls along the rows; each owner gets 1 to 20 rows and some owner exactly 20.
All inputs are finite; a program needn't handle non-finite values. No bound on the sum of `pixel_mask` on one device may be relied on, other than what follows from the above.
Results may differ from the reference program's by a relative error of at most 0.00007.
Values sent between devices are 32-bit elements; how exact they have to be, the bound alone decides.
No kernel may reach another device: no remote copies, remote signals or barrier semaphores. Data moves between devices by JAX's collectives and lax.ppermute only.
A program may use at most 128 MiB of HBM per device.

```python
import math
import jax
import jax.numpy as jnp
import numpy as np
from jax import lax

NCH = 256
PCOLS = 1024
NOUT = 256
CAP = 20
RMAX = 4
BW = 8
PROWS = 512
N_TILE = 16


def draw_radius(key, part):
    values = jax.random.randint(key, (NCH,), 1, RMAX + 1)
    chosen = jax.random.randint(jax.random.fold_in(key, 7), (), 0, NCH)
    return jnp.where(jnp.arange(NCH) == chosen, RMAX, values).astype(jnp.int32)


def plant(array, stream_key, low, largest):
    place = [jax.random.randint(jax.random.fold_in(stream_key, axis), (), 0, length) for axis, length in enumerate(array.shape)]
    main_axis = array.shape.index(max(array.shape))
    next_to = place[:main_axis] + [(place[main_axis] + 1) % array.shape[main_axis]] + place[main_axis + 1:]
    return array.at[tuple(place)].set(low).at[tuple(next_to)].set(largest)


def shard_levels(own_key, extent, shards, smallest, high):
    level = 1.0
    for axis_at, parts in shards:
        draws = jax.random.uniform(jax.random.fold_in(jax.random.fold_in(own_key, 6), axis_at), (parts,), jnp.float32, smallest / len(shards), high / len(shards))
        level = level * jnp.repeat(jnp.exp(draws), extent[axis_at] // parts).reshape((-1,) + (1,) * (len(extent) - 1 - axis_at))
    return level


def profile(amount, total, reach, lean):
    loads = [(1 << 20) // math.isqrt(grade ** lean) + 1 for grade in range(2, amount + 1)]
    spare, holding = total - reach - (amount - 1), [1] * (amount - 1)
    while spare > 0:
        free = [i for i in range(amount - 1) if holding[i] < reach]
        whole, remaining = sum([loads[i] for i in free]), spare
        for i in free:
            addition = min(reach - holding[i], max(1, remaining * loads[i] // whole), spare)
            holding[i] = holding[i] + addition
            spare = spare - addition
    return np.array([reach] + holding)


def ragged_sizes(stream_key, amount, total, reach, skew):
    if amount == 2:
        one = jax.random.randint(stream_key, (), max(1, total - reach), min(reach, total - 1) + 1)
        return jnp.stack([one, total - one])
    tallies = jnp.asarray(profile(amount, total, reach, skew), jnp.int32)
    couples = (amount - 1) // 2
    donor, receiver = tallies[1:1 + 2 * couples:2], tallies[2:2 + 2 * couples:2]
    slack = jnp.minimum(donor - 1, reach - receiver)
    moved = jax.random.randint(jax.random.fold_in(stream_key, 1), (couples,), 0, 1 << 20) % (slack + 1)
    tallies = tallies.at[1:1 + 2 * couples:2].set(donor - moved).at[2:2 + 2 * couples:2].set(receiver + moved)
    return tallies[jax.random.permutation(jax.random.fold_in(stream_key, 2), amount)]


def noise(stream_key, extent, scale, limit, cuts=(), kind=jnp.bfloat16):
    level = shard_levels(stream_key, extent, cuts, -0.22, 0.18) if cuts else 1.0
    drawn = jax.random.normal(stream_key, extent, jnp.float32) * scale * level
    return jnp.minimum(jnp.maximum(drawn, -limit), limit).astype(kind)


def setup_inputs(seed: int = 0) -> dict:
    key_of = jax.random.split(jax.random.key(seed), 8)
    return {
        "sky_cube": noise(key_of[0], (NCH, PROWS, PCOLS), 1.0, 8.0, ((0, 2), (1, 16)), jnp.float32),
        "pixel_mask": plant((jax.random.randint(key_of[1], (PROWS, PCOLS), 0, 10) < 9).astype(jnp.int32), jax.random.fold_in(key_of[1], 1), 0, 1),
        "radius": draw_radius(jax.random.fold_in(key_of[7], 71), 0),
        "chan_weight": jnp.clip(jnp.exp(jax.random.uniform(key_of[3], (NCH,), jnp.float32, math.log(0.5), math.log(2.0))), 0.5, 2.0),
        "band": jnp.clip(jax.random.uniform(key_of[4], (2 * BW + 1, NCH), jnp.float32, -0.15, 0.15), -0.15, 0.15),
        "resample": noise(key_of[5], (NOUT, NCH), NCH ** -0.5, 0.375, (), jnp.float32),
        "slab_index": jnp.searchsorted(jnp.cumsum(ragged_sizes(key_of[6], N_TILE, NOUT, CAP, 2)), jnp.arange(NOUT), side="right").astype(jnp.int32),
    }


def make_taps(radius):
    spread = radius.astype(jnp.float32)[:, None]
    offsets = jnp.arange(-RMAX, RMAX + 1).astype(jnp.float32)[None, :]
    sigma = 0.5 * spread + 0.5
    values = jnp.exp(-offsets * offsets / (2.0 * sigma * sigma))
    values = jnp.where(jnp.abs(offsets) <= spread, values, jnp.zeros_like(values))
    return values / jnp.sum(values, axis=1, keepdims=True)


def reference(sky_cube, pixel_mask, radius, chan_weight, band, resample, slab_index):
    taps = make_taps(radius)
    masked = sky_cube * pixel_mask.astype(sky_cube.dtype)[None]
    padded = jnp.pad(masked, ((0, 0), (RMAX, RMAX), (0, 0)))
    along_rows = jnp.zeros_like(masked)
    for offset in range(2 * RMAX + 1):
        along_rows = along_rows + taps[:, offset, None, None] * padded[:, offset:offset + PROWS, :]
    padded = jnp.pad(along_rows, ((0, 0), (0, 0), (RMAX, RMAX)))
    beam = jnp.zeros_like(masked)
    for offset in range(2 * RMAX + 1):
        beam = beam + taps[:, offset, None, None] * padded[:, :, offset:offset + PCOLS]
    weighted = chan_weight[:, None, None] * beam
    padded = jnp.pad(weighted, ((BW, BW), (0, 0), (0, 0)))
    filtered = weighted
    for offset in range(2 * BW + 1):
        filtered = filtered - band[offset][:, None, None] * padded[offset:offset + NCH]
    comoving = jnp.dot(resample, filtered.reshape(NCH, PROWS * PCOLS), precision=lax.Precision.HIGHEST, preferred_element_type=jnp.float32)
    owners = jnp.arange(N_TILE).astype(jnp.int32)
    onehot = (slab_index[None, :] == owners[:, None]).astype(jnp.int32)
    count = jnp.sum(onehot, axis=1).astype(jnp.int32)
    start = (jnp.cumsum(count) - count).astype(jnp.int32)
    slots = jnp.arange(CAP).astype(jnp.int32)
    source = (start[:, None] + slots[None, :]).astype(jnp.int32)
    valid = slots[None, :] < count[:, None]
    picked = jnp.take(comoving, jnp.clip(source, 0, NOUT - 1).reshape(-1), axis=0)
    picked = jnp.where(valid.reshape(-1)[:, None], picked, jnp.zeros_like(picked))
    return picked.reshape(N_TILE * CAP, PROWS, PCOLS)
```

```python
import jax
import jax.numpy as jnp
from jax import lax
from jax.experimental import pallas as pl
from jax.experimental.pallas import tpu as pltpu
from jax.sharding import PartitionSpec as P


CAP = 20
RMAX = 4
BW = 8
ROWS = 8
LANES = 128
SLOTS = 24
SUB = 256

LIGHT = pl.CostEstimate(flops=1, bytes_accessed=1, transcendentals=0)


def make_taps(radius):
    spread = radius.astype(jnp.float32)[:, None]
    offsets = jnp.arange(-RMAX, RMAX + 1).astype(jnp.float32)[None, :]
    sigma = 0.5 * spread + 0.5
    values = jnp.exp(-offsets * offsets / (2.0 * sigma * sigma))
    values = jnp.where(jnp.abs(offsets) <= spread, values, jnp.zeros_like(values))
    return (values / jnp.sum(values, axis=1, keepdims=True))[:, RMAX:]


def partner(index, step, count):
    if count & (count - 1) == 0:
        return index ^ step
    return (index + step) % count


def source_of(index, step, count):
    if count & (count - 1) == 0:
        return index ^ step
    return (index + count - step) % count


def shift(block, axis, step):
    count = lax.axis_size(axis)
    return lax.ppermute(block, axis, [(i, partner(i, step, count)) for i in range(count)])


def beam_kernel(above, below, first, last, count, col_width, pieces, waits, *refs):
    here_ref, taps_ref, prev_ref, cur_ref, next_ref, mprev_ref, mcur_ref, mnext_ref = refs[:8]
    outs = refs[8 + waits : -2]
    window, scratch = refs[-2:]
    group = cur_ref.shape[0]
    tiles = cur_ref.shape[2] // LANES
    base = pl.program_id(0) * group
    edges = list(outs[count * len(pieces) :])
    lane = lax.broadcasted_iota(jnp.int32, (ROWS, LANES), 1)
    zeros = jnp.zeros((ROWS, LANES), jnp.float32)

    def one(c, slot):
        taps = [taps_ref[(base + c) * (RMAX + 1) + k] for k in range(RMAX + 1)]
        sums = []
        for b in range(tiles):
            at = pl.ds(b * LANES, LANES)
            if above:
                window[slot, b, ROWS - RMAX : ROWS] = prev_ref[c, :, at]
            else:
                prev = prev_ref[c, :, at] * mprev_ref[:, at].astype(jnp.float32)
                window[slot, b, :ROWS] = prev
            window[slot, b, ROWS : 2 * ROWS] = cur_ref[c, :, at] * mcur_ref[:, at].astype(jnp.float32)
            if below:
                window[slot, b, 2 * ROWS : 2 * ROWS + RMAX] = next_ref[c, :, at]
            else:
                after = next_ref[c, :, at] * mnext_ref[:, at].astype(jnp.float32)
                window[slot, b, 2 * ROWS :] = after
            total = taps[0] * window[slot, b, ROWS : 2 * ROWS]
            for k in range(1, RMAX + 1):
                total = total + taps[k] * (
                    window[slot, b, ROWS - k : 2 * ROWS - k] + window[slot, b, ROWS + k : 2 * ROWS + k]
                )
            sums.append(total)
            if first:
                edges[0][c, :, at] = window[slot, b, :RMAX]
            if last:
                edges[-1][c, :, at] = window[slot, b, 3 * ROWS - RMAX :]
        totals = [taps[0] * total for total in sums]
        for k in range(1, RMAX + 1):
            right = [pltpu.roll(total, k, 1) for total in sums]
            left = [pltpu.roll(total, LANES - k, 1) for total in sums]
            for b in range(tiles):
                below_ = right[b - 1] if b else zeros
                above_ = left[b + 1] if b + 1 < tiles else zeros
                totals[b] = totals[b] + taps[k] * (
                    jnp.where(lane < k, below_, right[b])
                    + jnp.where(lane >= LANES - k, above_, left[b])
                )
        for b in range(tiles):
            scratch[c, :, pl.ds(b * LANES, LANES)] = totals[b]

    def pair(i, carry):
        one(2 * i, 0)
        one(2 * i + 1, 1)
        return carry

    lax.fori_loop(0, group // 2, pair, 0)
    me = here_ref[0]
    at = 0
    for step in range(count):
        start = partner(me, step, count) * col_width
        for col, width in pieces:
            outs[at][...] = scratch[:, :, pl.ds(pl.multiple_of(start + col, LANES), width)]
            at += 1


def beam_block(sky, mask, up, down, taps, me, block, count, pieces, after):
    chans, rows, cols = sky.shape
    blocks = rows // ROWS
    above, below = block == 0, block == blocks - 1
    first, last = block == 1 and blocks > 2, block == blocks - 2 and blocks > 2
    group = min(chans, 16)
    col_width = cols // count
    full = lambda b: pl.BlockSpec((group, ROWS, cols), lambda i: (i, b, 0))
    half = pl.BlockSpec((group, RMAX, cols), lambda i: (i, 0, 0))
    mrow = lambda b: pl.BlockSpec((ROWS, cols), lambda i: (b, 0))
    lo, hi = max(block - 1, 0), min(block + 1, blocks - 1)
    smem = pl.BlockSpec(memory_space=pltpu.SMEM)
    out_specs, out_shapes = [], []
    for _ in range(count):
        for _, width in pieces:
            out_specs.append(pl.BlockSpec((group, ROWS, width), lambda i: (i, 0, 0)))
            out_shapes.append(jax.ShapeDtypeStruct((chans, ROWS, width), jnp.float32))
    for _ in range(first + last):
        out_specs.append(half)
        out_shapes.append(jax.ShapeDtypeStruct((chans, RMAX, cols), jnp.float32))
    return pl.pallas_call(
        lambda *refs: beam_kernel(
            above, below, first, last, count, col_width, pieces, len(after), *refs
        ),
        grid=(chans // group,),
        in_specs=[
            smem,
            smem,
            half if above else full(lo),
            full(block),
            half if below else full(hi),
            mrow(lo),
            mrow(block),
            mrow(hi),
        ]
        + [pl.BlockSpec(memory_space=pl.ANY)] * len(after),
        out_specs=out_specs,
        out_shape=out_shapes,
        scratch_shapes=[
            pltpu.VMEM((2, cols // LANES, 3 * ROWS, LANES), jnp.float32),
            pltpu.VMEM((group, ROWS, cols), jnp.float32),
        ],
        cost_estimate=LIGHT,
        name="beam",
    )(me, taps, up if above else sky, sky, down if below else sky, mask, mask, mask, *after)


def mix_kernel(count, owners, waits, weights_ref, *refs):
    parts, outs = refs[:count], refs[count + waits :]
    chans = parts[0].shape[0]
    columns = []
    for part in parts:
        flat = part.reshape(chans * ROWS, LANES)
        columns.append(
            jnp.concatenate([flat[pl.ds(r, chans, stride=ROWS), :] for r in range(ROWS)], axis=1)
        )
    values = jnp.concatenate(columns, axis=0)
    high = values.astype(jnp.bfloat16)
    low = (values - high.astype(jnp.float32)).astype(jnp.bfloat16)
    mixed = jnp.dot(
        weights_ref[...],
        jnp.concatenate([high, high, low], axis=0),
        preferred_element_type=jnp.float32,
    )
    for o in range(owners):
        flat = outs[o].reshape(CAP * ROWS, LANES)
        for r in range(ROWS):
            flat[pl.ds(r, CAP, stride=ROWS), :] = mixed[
                o * SLOTS : o * SLOTS + CAP, r * LANES : (r + 1) * LANES
            ]


def mix(weights, parts, owners, after):
    count = len(parts)
    chans, _, width = parts[0].shape
    k = weights.shape[0] * weights.shape[1] * ROWS * width
    return pl.pallas_call(
        lambda *refs: mix_kernel(count, owners, len(after), *refs),
        grid=(width // LANES,),
        in_specs=[pl.BlockSpec(weights.shape, lambda j: (0, 0))]
        + [pl.BlockSpec((chans, ROWS, LANES), lambda j: (0, 0, j))] * count
        + [pl.BlockSpec(memory_space=pl.ANY)] * len(after),
        out_specs=[pl.BlockSpec((CAP, ROWS, LANES), lambda j: (0, 0, j))] * owners,
        out_shape=[jax.ShapeDtypeStruct((CAP, ROWS, width), jnp.float32)] * owners,
        cost_estimate=pl.CostEstimate(
            flops=2 * k, bytes_accessed=4 * ROWS * width * (count * chans + owners * CAP), transcendentals=0
        ),
        name="mix",
    )(weights, *parts, *after)


def place_kernel(owners, rows, block, col, width, aliased, here_ref, *refs):
    arrived = refs[:owners][::-1]
    out, buffer, sems = refs[owners + aliased :]
    me = here_ref[0]
    loads = [pltpu.make_async_copy(arrived[m], buffer.at[m], sems.at[m]) for m in range(owners)]
    for load in loads:
        load.start()
    stores = []
    for m in range(owners):
        loads[m].wait()
        row = pl.multiple_of(source_of(me, m, owners) * rows + block * ROWS, ROWS)
        store = pltpu.make_async_copy(
            buffer.at[m], out.at[:, pl.ds(row, ROWS), pl.ds(col, width)], sems.at[owners + m]
        )
        store.start()
        stores.append(store)
    for store in stores:
        store.wait()


def place(result, shape, arrived, me, rows, block, col):
    owners = len(arrived)
    width = arrived[0].shape[2]
    aliased = 0 if result is None else 1
    anywhere = pl.BlockSpec(memory_space=pl.ANY)
    return pl.pallas_call(
        lambda *refs: place_kernel(owners, rows, block, col, width, aliased, *refs),
        in_specs=[pl.BlockSpec(memory_space=pltpu.SMEM)] + [anywhere] * (owners + aliased),
        out_specs=anywhere,
        out_shape=jax.ShapeDtypeStruct(shape, jnp.float32),
        scratch_shapes=[
            pltpu.VMEM((owners, CAP, ROWS, width), jnp.float32),
            pltpu.SemaphoreType.DMA((2 * owners,)),
        ],
        input_output_aliases={owners + 1: 0} if aliased else {},
        cost_estimate=LIGHT,
        name="place",
    )(me, *arrived[::-1], *([result] if aliased else []))


def mixing_weights(resample, band, chan_weight, slab_index, me_chan, me_tile, chans, owners):
    nch = resample.shape[1]
    row_ids = jnp.arange(nch)[:, None]
    col_ids = jnp.arange(nch)[None, :]
    distance = col_ids - row_ids
    coupling = jnp.zeros((nch, nch), jnp.float32)
    for offset in range(2 * BW + 1):
        coupling = coupling + jnp.where(distance == offset - BW, band[offset][:, None], 0.0)
    identity = (distance == 0).astype(jnp.float32)
    filter_matrix = (identity - coupling) * chan_weight[None, :]
    joined = jnp.dot(
        resample, filter_matrix, precision=lax.Precision.HIGHEST, preferred_element_type=jnp.float32
    )
    line = jnp.arange(owners * SLOTS)
    owner = partner(me_tile, line // SLOTS, owners)
    slot = line % SLOTS
    start = jnp.sum((slab_index[None, :] < owner[:, None]).astype(jnp.int32), axis=1)
    row = jnp.arange(resample.shape[0])[None, :]
    chosen = (
        (slab_index[None, :] == owner[:, None])
        & (row - start[:, None] == slot[:, None])
        & (slot[:, None] < CAP)
    ).astype(jnp.float32)
    count = nch // chans
    order = jnp.concatenate(
        [
            lax.dynamic_slice_in_dim(joined, source_of(me_chan, step, count) * chans, chans, axis=1)
            for step in range(count)
        ],
        axis=1,
    )
    weights = jnp.dot(
        chosen, order, precision=lax.Precision.HIGHEST, preferred_element_type=jnp.float32
    )
    high = lax.reduce_precision(weights, exponent_bits=8, mantissa_bits=7)
    low = weights - high
    return jnp.concatenate([high, low, high], axis=1).astype(jnp.bfloat16)


def body(sky_cube, pixel_mask, radius, chan_weight, band, resample, slab_index):
    chans, rows, cols = sky_cube.shape
    nchan, owners = lax.axis_size("chan"), lax.axis_size("tile")
    me_chan, me_tile = lax.axis_index("chan"), lax.axis_index("tile")
    col_width = cols // nchan
    blocks = rows // ROWS

    taps = make_taps(lax.dynamic_slice_in_dim(radius, me_chan * chans, chans)).reshape(-1)
    here_chan = jnp.reshape(me_chan, (1,)).astype(jnp.int32)
    here_tile = jnp.reshape(me_tile, (1,)).astype(jnp.int32)

    sub = min(SUB, col_width)
    fine = tuple((c, sub) for c in range(0, col_width, sub))
    whole = ((0, col_width),)
    order = list(range(1, blocks - 1)) + [0] + ([blocks - 1] if blocks > 1 else [])
    weights = mixing_weights(
        resample, band, chan_weight, slab_index, me_chan, me_tile, chans, owners
    )
    shape = (CAP, owners * rows, col_width)
    forward = [(i, i + 1) for i in range(owners - 1)]
    backward = [(b, a) for a, b in forward]
    edges = {}
    if blocks <= 2:
        mask = pixel_mask.astype(jnp.float32)[None]
        edges["first"] = sky_cube[:, :RMAX] * mask[:, :RMAX]
        edges["last"] = sky_cube[:, rows - RMAX :] * mask[:, rows - RMAX :]
    up = down = result = None
    mixed, placed = [], []
    for at, block in enumerate(order):
        pieces = fine if at in (0, len(order) - 1) else whole
        after = mixed[at - 2 : at - 1] if at >= 2 else []
        if block == 0 and up is None:
            up = lax.ppermute(edges["last"], "tile", forward)
        if block == blocks - 1 and down is None:
            down = lax.ppermute(edges["first"], "tile", backward)
        cut = beam_block(sky_cube, pixel_mask, up, down, taps, here_chan, block, nchan, pieces, after)
        extra = list(cut[nchan * len(pieces) :])
        if blocks > 2 and block == 1:
            edges["first"] = extra[0]
        if blocks > 2 and block == blocks - 2:
            edges["last"] = extra[-1]
        for j, (col, _) in enumerate(pieces):
            parts = [cut[j]]
            for step in range(1, nchan):
                parts.append(shift(cut[step * len(pieces) + j], "chan", step))
            outgoing = mix(weights, parts, owners, placed[-2:-1])
            mixed.append(outgoing[0])
            arrived = {0: outgoing[0]}
            for m in range(owners - 1, 0, -1):
                arrived[m] = shift(outgoing[m], "tile", m)
            arrived = [arrived[m] for m in range(owners)]
            result = place(result, shape, arrived, here_tile, rows, block, col)
            placed.append(result)
    return result


def solution(mesh):
    in_specs = (P("chan", "tile", None), P("tile", None), P(), P(), P(), P(), P())
    out_specs = P("tile", None, "chan")

    return jax.shard_map(body, mesh=mesh, in_specs=in_specs, out_specs=out_specs, check_vma=False)
```

```python
import jax
import jax.numpy as jnp
from jax import lax
from jax.experimental import pallas as pl
from jax.experimental.pallas import tpu as pltpu
from jax.sharding import PartitionSpec as P


CAP = 20
RMAX = 4
BW = 8
ROWS = 8
LANES = 128
SLOTS = 24
SUB = 256

LIGHT = pl.CostEstimate(flops=1, bytes_accessed=1, transcendentals=0)


def make_taps(radius):
    spread = radius.astype(jnp.float32)[:, None]
    offsets = jnp.arange(-RMAX, RMAX + 1).astype(jnp.float32)[None, :]
    sigma = 0.5 * spread + 0.5
    values = jnp.exp(-offsets * offsets / (2.0 * sigma * sigma))
    values = jnp.where(jnp.abs(offsets) <= spread, values, jnp.zeros_like(values))
    return (values / jnp.sum(values, axis=1, keepdims=True))[:, RMAX:]


def partner(index, step, count):
    if count & (count - 1) == 0:
        return index ^ step
    return (index + step) % count


def source_of(index, step, count):
    if count & (count - 1) == 0:
        return index ^ step
    return (index + count - step) % count


def shift(block, axis, step):
    count = lax.axis_size(axis)
    return lax.ppermute(block, axis, [(i, partner(i, step, count)) for i in range(count)])


def beam_kernel(above, below, first, last, count, col_width, pieces, waits, *refs):
    here_ref, taps_ref, prev_ref, cur_ref, next_ref, mprev_ref, mcur_ref, mnext_ref = refs[:8]
    outs = refs[8 + waits : -3]
    masks, window, scratch = refs[-3:]
    group = cur_ref.shape[0]
    tiles = cur_ref.shape[2] // LANES
    base = pl.program_id(0) * group
    edges = list(outs[count * len(pieces) :])
    narrow = sorted(
        (owner * col_width + col) // LANES + j
        for owner in range(count)
        for col, width in pieces
        for j in range(width // LANES)
    )
    wide = sorted({b + j for b in narrow for j in (-1, 0, 1)} & set(range(tiles)))
    lane = lax.broadcasted_iota(jnp.int32, (ROWS, LANES), 1)

    @pl.when(pl.program_id(0) == 0)
    def _():
        for j, ref in enumerate((mprev_ref, mcur_ref, mnext_ref)):
            masks[j] = ref[...].astype(jnp.float32)

    def along_rows(c, slot):
        taps = [taps_ref[(base + c) * (RMAX + 1) + k] for k in range(RMAX + 1)]
        sums = []
        for b in wide if not edges else range(tiles):
            at = pl.ds(b * LANES, LANES)

            def rows(start, size):
                return pl.ds(2 * ((slot * tiles + b) * 3 * ROWS + start), size, stride=2)

            if above:
                window[rows(ROWS - RMAX, RMAX)] = prev_ref[c, :, at]
            else:
                prev = prev_ref[c, :, at] * masks[0, :, at]
                window[rows(0, ROWS)] = prev
                if first:
                    edges[0][c, :, at] = prev[:RMAX]
            cur = cur_ref[c, :, at] * masks[1, :, at]
            window[rows(ROWS, ROWS)] = cur
            if below:
                window[rows(2 * ROWS, RMAX)] = next_ref[c, :, at]
            else:
                after = next_ref[c, :, at] * masks[2, :, at]
                window[rows(2 * ROWS, ROWS)] = after
                if last:
                    edges[-1][c, :, at] = after[ROWS - RMAX :]
            total = taps[0] * cur
            for k in range(1, RMAX + 1):
                total = total + taps[k] * (
                    window[rows(ROWS - k, ROWS)] + window[rows(ROWS + k, ROWS)]
                )
            sums.append(total)
        return sums

    def along_cols(c, sums):
        t = [taps_ref[(base + c) * (RMAX + 1) + k] for k in range(RMAX + 1)]
        x = dict(zip(wide if not edges else range(tiles), sums))
        right = {b: pltpu.roll(v, 1, 1) for b, v in x.items()}
        left = {b: pltpu.roll(v, LANES - 1, 1) for b, v in x.items()}
        low, high, middle = {}, {}, {}
        for b in x:
            before = jnp.where(lane < 1, right.get(b - 1, 0.0), right[b])
            after = jnp.where(lane >= LANES - 1, left.get(b + 1, 0.0), left[b])
            if b in narrow or b + 1 in narrow:
                low[b] = t[4] * before + t[3] * x[b] + t[2] * after
            if b in narrow:
                middle[b] = t[1] * (before + after) + t[0] * x[b]
            if b in narrow or b - 1 in narrow:
                high[b] = t[2] * before + t[3] * x[b] + t[4] * after
        if 0 in narrow:
            low[-1] = jnp.where(lane >= LANES - 1, t[2] * left[0], 0.0)
        if tiles - 1 in narrow:
            high[tiles] = jnp.where(lane < 1, t[2] * right[tiles - 1], 0.0)
        low = {b: pltpu.roll(v, 3, 1) for b, v in low.items()}
        high = {b: pltpu.roll(v, LANES - 3, 1) for b, v in high.items()}
        for b in narrow:
            before = jnp.where(lane < 3, low[b - 1], low[b])
            after = jnp.where(lane >= LANES - 3, high[b + 1], high[b])
            scratch[c, :, pl.ds(b * LANES, LANES)] = middle[b] + (before + after)

    def step(i, sums):
        following = along_rows(2 * i + 2, 0), along_rows(2 * i + 3, 1)
        along_cols(2 * i, sums[0])
        along_cols(2 * i + 1, sums[1])
        return following

    start = along_rows(0, 0), along_rows(1, 1)
    sums = lax.fori_loop(0, group // 2 - 1, step, start)
    along_cols(group - 2, sums[0])
    along_cols(group - 1, sums[1])
    me = here_ref[0]
    at = 0
    for step in range(count):
        start = partner(me, step, count) * col_width
        for col, width in pieces:
            outs[at][...] = scratch[:, :, pl.ds(pl.multiple_of(start + col, LANES), width)]
            at += 1


def beam_block(sky, mask, up, down, taps, me, block, count, pieces, edges, after):
    chans, rows, cols = sky.shape
    blocks = rows // ROWS
    above, below = block == 0, block == blocks - 1
    first, last = edges and block == 1 and blocks > 2, edges and block == blocks - 2 and blocks > 2
    group = min(chans, 16)
    col_width = cols // count
    full = lambda b: pl.BlockSpec((group, ROWS, cols), lambda i: (i, b, 0))
    half = pl.BlockSpec((group, RMAX, cols), lambda i: (i, 0, 0))
    mrow = lambda b: pl.BlockSpec((ROWS, cols), lambda i: (b, 0))
    lo, hi = max(block - 1, 0), min(block + 1, blocks - 1)
    smem = pl.BlockSpec(memory_space=pltpu.SMEM)
    out_specs, out_shapes = [], []
    for _ in range(count):
        for _, width in pieces:
            out_specs.append(pl.BlockSpec((group, ROWS, width), lambda i: (i, 0, 0)))
            out_shapes.append(jax.ShapeDtypeStruct((chans, ROWS, width), jnp.float32))
    for _ in range(first + last):
        out_specs.append(half)
        out_shapes.append(jax.ShapeDtypeStruct((chans, RMAX, cols), jnp.float32))
    return pl.pallas_call(
        lambda *refs: beam_kernel(
            above, below, first, last, count, col_width, pieces, len(after), *refs
        ),
        grid=(chans // group,),
        in_specs=[
            smem,
            smem,
            half if above else full(lo),
            full(block),
            half if below else full(hi),
            mrow(lo),
            mrow(block),
            mrow(hi),
        ]
        + [pl.BlockSpec(memory_space=pl.ANY)] * len(after),
        out_specs=out_specs,
        out_shape=out_shapes,
        scratch_shapes=[
            pltpu.VMEM((3, ROWS, cols), jnp.float32),
            pltpu.VMEM((2 * cols // LANES * 6 * ROWS, LANES), jnp.float32),
            pltpu.VMEM((group, ROWS, cols), jnp.float32),
        ],
        cost_estimate=LIGHT,
        name="beam",
    )(me, taps, up if above else sky, sky, down if below else sky, mask, mask, mask, *after)


def mix_kernel(count, owners, waits, weights_ref, *refs):
    parts, outs = refs[:count], refs[count + waits :]
    chans = parts[0].shape[0]
    columns = []
    for part in parts:
        flat = part.reshape(chans * ROWS, LANES)
        columns.append(
            jnp.concatenate([flat[pl.ds(r, chans, stride=ROWS), :] for r in range(ROWS)], axis=1)
        )
    values = jnp.concatenate(columns, axis=0)
    high = values.astype(jnp.bfloat16)
    low = (values - high.astype(jnp.float32)).astype(jnp.bfloat16)
    mixed = jnp.dot(
        weights_ref[...],
        jnp.concatenate([high, high, low], axis=0),
        preferred_element_type=jnp.float32,
    )
    for o in range(owners):
        flat = outs[o].reshape(CAP * ROWS, LANES)
        for r in range(ROWS):
            flat[pl.ds(r, CAP, stride=ROWS), :] = mixed[
                o * SLOTS : o * SLOTS + CAP, r * LANES : (r + 1) * LANES
            ]


def mix(weights, parts, owners, after):
    count = len(parts)
    chans, _, width = parts[0].shape
    k = weights.shape[0] * weights.shape[1] * ROWS * width
    return pl.pallas_call(
        lambda *refs: mix_kernel(count, owners, len(after), *refs),
        grid=(width // LANES,),
        in_specs=[pl.BlockSpec(weights.shape, lambda j: (0, 0))]
        + [pl.BlockSpec((chans, ROWS, LANES), lambda j: (0, 0, j))] * count
        + [pl.BlockSpec(memory_space=pl.ANY)] * len(after),
        out_specs=[pl.BlockSpec((CAP, ROWS, LANES), lambda j: (0, 0, j))] * owners,
        out_shape=[jax.ShapeDtypeStruct((CAP, ROWS, width), jnp.float32)] * owners,
        cost_estimate=pl.CostEstimate(
            flops=2 * k, bytes_accessed=4 * ROWS * width * (count * chans + owners * CAP), transcendentals=0
        ),
        name="mix",
    )(weights, *parts, *after)


def place_kernel(owners, rows, block, col, width, aliased, here_ref, *refs):
    arrived = refs[:owners][::-1]
    out, buffer, sems = refs[owners + aliased :]
    me = here_ref[0]
    loads = [pltpu.make_async_copy(arrived[m], buffer.at[m], sems.at[m]) for m in range(owners)]
    for load in loads:
        load.start()
    stores = []
    for m in range(owners):
        loads[m].wait()
        row = pl.multiple_of(source_of(me, m, owners) * rows + block * ROWS, ROWS)
        store = pltpu.make_async_copy(
            buffer.at[m], out.at[:, pl.ds(row, ROWS), pl.ds(col, width)], sems.at[owners + m]
        )
        store.start()
        stores.append(store)
    for store in stores:
        store.wait()


def place(result, shape, arrived, me, rows, block, col):
    owners = len(arrived)
    width = arrived[0].shape[2]
    aliased = 0 if result is None else 1
    anywhere = pl.BlockSpec(memory_space=pl.ANY)
    return pl.pallas_call(
        lambda *refs: place_kernel(owners, rows, block, col, width, aliased, *refs),
        in_specs=[pl.BlockSpec(memory_space=pltpu.SMEM)] + [anywhere] * (owners + aliased),
        out_specs=anywhere,
        out_shape=jax.ShapeDtypeStruct(shape, jnp.float32),
        scratch_shapes=[
            pltpu.VMEM((owners, CAP, ROWS, width), jnp.float32),
            pltpu.SemaphoreType.DMA((2 * owners,)),
        ],
        input_output_aliases={owners + 1: 0} if aliased else {},
        cost_estimate=LIGHT,
        name="place",
    )(me, *arrived[::-1], *([result] if aliased else []))


def mixing_weights(resample, band, chan_weight, slab_index, me_chan, me_tile, chans, owners):
    nch = resample.shape[1]
    row_ids = jnp.arange(nch)[:, None]
    col_ids = jnp.arange(nch)[None, :]
    distance = col_ids - row_ids
    coupling = jnp.zeros((nch, nch), jnp.float32)
    for offset in range(2 * BW + 1):
        coupling = coupling + jnp.where(distance == offset - BW, band[offset][:, None], 0.0)
    identity = (distance == 0).astype(jnp.float32)
    filter_matrix = (identity - coupling) * chan_weight[None, :]
    joined = jnp.dot(
        resample, filter_matrix, precision=lax.Precision.HIGHEST, preferred_element_type=jnp.float32
    )
    line = jnp.arange(owners * SLOTS)
    owner = partner(me_tile, line // SLOTS, owners)
    slot = line % SLOTS
    start = jnp.sum((slab_index[None, :] < owner[:, None]).astype(jnp.int32), axis=1)
    row = jnp.arange(resample.shape[0])[None, :]
    chosen = (
        (slab_index[None, :] == owner[:, None])
        & (row - start[:, None] == slot[:, None])
        & (slot[:, None] < CAP)
    ).astype(jnp.float32)
    count = nch // chans
    order = jnp.concatenate(
        [
            lax.dynamic_slice_in_dim(joined, source_of(me_chan, step, count) * chans, chans, axis=1)
            for step in range(count)
        ],
        axis=1,
    )
    weights = jnp.dot(
        chosen, order, precision=lax.Precision.HIGHEST, preferred_element_type=jnp.float32
    )
    high = lax.reduce_precision(weights, exponent_bits=8, mantissa_bits=7)
    low = weights - high
    return jnp.concatenate([high, low, high], axis=1).astype(jnp.bfloat16)


def body(sky_cube, pixel_mask, radius, chan_weight, band, resample, slab_index):
    chans, rows, cols = sky_cube.shape
    nchan, owners = lax.axis_size("chan"), lax.axis_size("tile")
    me_chan, me_tile = lax.axis_index("chan"), lax.axis_index("tile")
    col_width = cols // nchan
    blocks = rows // ROWS

    taps = make_taps(lax.dynamic_slice_in_dim(radius, me_chan * chans, chans)).reshape(-1)
    here_chan = jnp.reshape(me_chan, (1,)).astype(jnp.int32)
    here_tile = jnp.reshape(me_tile, (1,)).astype(jnp.int32)

    sub = min(SUB, col_width)
    fine = tuple((c, sub) for c in range(0, col_width, sub))
    whole = ((0, col_width),)
    order = list(range(1, blocks - 1)) + [0] + ([blocks - 1] if blocks > 1 else [])
    weights = mixing_weights(
        resample, band, chan_weight, slab_index, me_chan, me_tile, chans, owners
    )
    shape = (CAP, owners * rows, col_width)
    forward = [(i, i + 1) for i in range(owners - 1)]
    backward = [(b, a) for a, b in forward]
    edges = {}
    if blocks <= 2:
        mask = pixel_mask.astype(jnp.float32)[None]
        edges["first"] = sky_cube[:, :RMAX] * mask[:, :RMAX]
        edges["last"] = sky_cube[:, rows - RMAX :] * mask[:, rows - RMAX :]
    up = down = result = None
    calls = [
        (block, fine if block in (order[0], order[-1]) else whole, True) for block in order
    ]
    mixed, placed = [], []
    for at, (block, pieces, sides) in enumerate(calls):
        after = mixed[:1] if at >= 2 else []
        if block == 0 and up is None:
            up = lax.ppermute(edges["last"], "tile", forward)
        if block == blocks - 1 and down is None:
            down = lax.ppermute(edges["first"], "tile", backward)
        cut = beam_block(
            sky_cube, pixel_mask, up, down, taps, here_chan, block, nchan, pieces, sides, after
        )
        extra = list(cut[nchan * len(pieces) :])
        if extra and block == 1:
            edges["first"] = extra[0]
        if extra and block == blocks - 2:
            edges["last"] = extra[-1]
        for j, (col, _) in enumerate(pieces):
            parts = [cut[j]]
            for step in range(1, nchan):
                parts.append(shift(cut[step * len(pieces) + j], "chan", step))
            outgoing = mix(weights, parts, owners, placed[-2:-1])
            mixed.append(outgoing[0])
            arrived = {0: outgoing[0]}
            for m in range(owners - 1, 0, -1):
                arrived[m] = shift(outgoing[m], "tile", m)
            arrived = [arrived[m] for m in range(owners)]
            result = place(result, shape, arrived, here_tile, rows, block, col)
            placed.append(result)
    return result


def solution(mesh):
    in_specs = (P("chan", "tile", None), P("tile", None), P(), P(), P(), P(), P())
    out_specs = P("tile", None, "chan")

    return jax.shard_map(body, mesh=mesh, in_specs=in_specs, out_specs=out_specs, check_vma=False)
```
